32 devices in a mesh: shot: 8 (over z, y), point: 4 (over x, core).
Axes of the slice: x: 2, y: 2, z: 4, core: 2. Of those that a mesh axis runs over, the one named last changes fastest.
Arguments:
- traces: bfloat16 [16, 8, 1024], P('shot', 'point'), may hold values from -6 to 6
- panels: bfloat16 [8, 256, 1024], P('point', 'shot'), may hold values from -0.125 to 0.125
- aperture: int32 [16, 8], P('shot', 'point'), may hold values 0 or 1
- window_lo: int32 [256, 16], P('point', 'shot'), may hold values from 0 to 255
- window_hi: int32 [256, 16], P('point', 'shot'), may hold values from 512 to 1023
Outputs:
- multiples: bfloat16 [256, 16, 1024], P('point', 'shot')
The draws below stay inside these ranges and needn't reach their ends.
All inputs are finite; a program needn't handle non-finite values. No bound on the sum of `aperture` on one device may be relied on, other than what follows from the above.
Results may differ from the reference program's by a relative error of at most 0.001.
Values may be sent and summed in bfloat16 or wider, within the bound.
No kernel may reach another device: no remote copies, remote signals or barrier semaphores. Data moves between devices by JAX's collectives and lax.ppermute only.
A program may use at most 64 MiB of HBM per device.

```python
import jax
import jax.numpy as jnp
from jax import lax

RECEIVERS = 256
SAMPLES = 1024
POINTS = 8
SHOTS = 16


def with_ends(array, rng, least, high):
    index_at = [jax.random.randint(jax.random.fold_in(rng, axis), (), 0, length) for axis, length in enumerate(array.shape)]
    main_axis = array.shape.index(max(array.shape))
    beside = index_at[:main_axis] + [(index_at[main_axis] + 1) % array.shape[main_axis]] + index_at[main_axis + 1:]
    return array.at[tuple(index_at)].set(least).at[tuple(beside)].set(high)


def with_spikes(drawn, rng, source, target, shards_of, factor):
    owner, partner = [(jnp.arange(drawn.shape[axis_at]) // (drawn.shape[axis_at] // shards_of)).reshape([-1 if axis == axis_at else 1 for axis in range(drawn.ndim)]) for axis_at in (source, target)]
    chosen = jax.random.permutation(rng, shards_of)[partner]
    strong = (owner == chosen) | (owner == (partner + shards_of // 2) % shards_of)
    return jnp.where(strong, factor * drawn, drawn)


def steps_of(stream_key, extent, split, smallest, largest):
    def one(dim, parts):
        heights = jax.random.uniform(jax.random.fold_in(jax.random.fold_in(stream_key, 6), dim), (parts,), jnp.float32, smallest / len(split), largest / len(split))
        return jnp.repeat(jnp.exp(heights), extent[dim] // parts).reshape((-1,) + (1,) * (len(extent) - dim - 1))

    factor_of = one(*split[0])
    for cut in split[1:]:
        factor_of = factor_of * one(*cut)
    return factor_of


def normal_values(own_key, shape, width, reach, split=(), kind=jnp.bfloat16):
    loudness = steps_of(own_key, shape, split, -0.22, 0.18) if split else 1.0
    result = jax.random.normal(own_key, shape, jnp.float32) * width * loudness
    return jnp.minimum(jnp.maximum(result, -reach), reach).astype(kind)


def bell_draw_with(stream_key, extent, spread, limit, cuts, heavy, kind=jnp.bfloat16):
    result = spread * jax.random.normal(stream_key, extent, jnp.float32)
    if cuts:
        result = result * steps_of(stream_key, extent, cuts, -0.22, 0.18)
    return jnp.clip(with_spikes(result, jax.random.fold_in(stream_key, 3), *heavy), -limit, limit).astype(kind)


def setup_inputs(seed: int = 0) -> dict:
    key_list = jax.random.split(jax.random.key(seed), 6)
    return {
        "traces": normal_values(key_list[0], (SHOTS, POINTS, SAMPLES), 1.0, 6.0, ((0, 8), (1, 4))),
        "panels": bell_draw_with(key_list[1], (POINTS, RECEIVERS, SAMPLES), (POINTS * SAMPLES // 2) ** -0.5, 0.125, ((0, 4), (1, 8)), (0, 1, 8, 2.0)),
        "aperture": with_ends((jax.random.randint(key_list[2], (SHOTS, POINTS), 0, 4) < 3).astype(jnp.int32), jax.random.fold_in(key_list[2], 1), 0, 1),
        "window_lo": with_ends(jax.random.randint(key_list[3], (RECEIVERS, SHOTS), 0, SAMPLES // 4), jax.random.fold_in(key_list[3], 1), 0, (SAMPLES // 4) - 1).astype(jnp.int32),
        "window_hi": with_ends(jax.random.randint(key_list[4], (RECEIVERS, SHOTS), SAMPLES // 2, SAMPLES), jax.random.fold_in(key_list[4], 1), SAMPLES // 2, SAMPLES - 1).astype(jnp.int32),
    }


def toeplitz(series):
    count = series.shape[-1]
    padded = jnp.concatenate([series, jnp.zeros_like(series)], -1)
    tiled_flat = jnp.tile(padded, (1, count))[:, :count * (2 * count - 1)]
    return tiled_flat.reshape(series.shape[0], count, 2 * count - 1)[:, :, :count]


def window_weights(window_lo, window_hi, length):
    sample_axis = jnp.arange(length).astype(jnp.float32)[None, None, :]
    lower = window_lo.astype(jnp.float32)[:, :, None]
    upper = window_hi.astype(jnp.float32)[:, :, None]
    rising = jnp.clip((sample_axis - lower + 32.0) / 32.0, 0.0, 1.0)
    falling = jnp.clip((upper - sample_axis) / 32.0, 0.0, 1.0)
    return rising * falling


def reference(traces, panels, aperture, window_lo, window_hi):
    masked = traces * aperture[:, :, None].astype(traces.dtype)

    def one_point(point, total_sum):
        series = lax.dynamic_index_in_dim(masked, point, 1, keepdims=False)
        kernel = toeplitz(series).astype(jnp.float32)
        panel_rows = lax.dynamic_index_in_dim(panels, point, 0, keepdims=False).astype(jnp.float32)
        return total_sum + jnp.einsum("ru,sut->rst", panel_rows, kernel)

    initial = jnp.zeros((panels.shape[1], traces.shape[0], traces.shape[2]), jnp.float32)
    predicted = lax.fori_loop(0, panels.shape[0], one_point, initial)
    weights = window_weights(window_lo, window_hi, traces.shape[2])
    return (weights * predicted).astype(jnp.bfloat16)
```

```python
import functools

import jax
import jax.numpy as jnp
from jax import lax
from jax.experimental import pallas as pl
from jax.experimental.pallas import tpu as pltpu
from jax.sharding import PartitionSpec as P


LANES = 128
WIDTH = 256

AXES = ("shot", "point")


def convolve_kernel(count, order_ref, *refs):
    panel_refs = refs[:count]
    trace_ref, near_lo, near_hi, far_lo, far_hi, near_out, far_out, left, right, total = refs[count:]
    row, local_points = order_ref[count], panel_refs[0].shape[0]
    receivers, length = panel_refs[0].shape[1:]
    local_shots = near_out.shape[0]
    blocks = length // LANES

    for k in range(count):
        for p in range(local_points):
            column = (k * local_points + p) * LANES
            pieces = [
                panel_refs[k][p, :, u * LANES : (u + 1) * LANES].astype(jnp.float32)
                for u in range(blocks)
            ]
            left[:, column : column + LANES] = jnp.concatenate(pieces, 0).astype(jnp.bfloat16)

    lag = lax.broadcasted_iota(jnp.int32, (LANES, LANES), 0)
    sample = lax.broadcasted_iota(jnp.int32, (LANES, LANES), 1)
    causal = sample >= lag
    axis = lax.broadcasted_iota(jnp.int32, (receivers, length), 1).astype(jnp.float32)
    first_row = pl.multiple_of(row * receivers, receivers)

    for side, (lo_ref, hi_ref, out_ref) in enumerate(
        ((far_lo, far_hi, far_out), (near_lo, near_hi, near_out))
    ):
        for s in range(local_shots):
            for k in range(count):
                for p in range(local_points):
                    at = (k * local_points + p) * LANES
                    series = trace_ref[order_ref[k], 1 - side, s, p : p + 1, :].astype(jnp.float32)
                    spread = jnp.broadcast_to(series, (LANES, length))
                    turned = pltpu.roll(spread, 0, 1, stride=1, stride_axis=0)
                    right[at : at + LANES, :] = turned.astype(jnp.bfloat16)
                    right[at : at + LANES, :LANES] = jnp.where(
                        causal, turned[:, :LANES], 0.0
                    ).astype(jnp.bfloat16)
            total[...] = jnp.zeros_like(total)
            for start in range(0, length, WIDTH):
                kept = (length - start) // LANES
                product = jnp.dot(
                    left[: kept * receivers, :],
                    right[:, start : start + WIDTH],
                    preferred_element_type=jnp.float32,
                )
                for u in range(kept):
                    here = slice(u * LANES + start, u * LANES + start + WIDTH)
                    total[:, here] += product[u * receivers : (u + 1) * receivers]
            lower = lo_ref[pl.ds(first_row, receivers), s : s + 1].astype(jnp.float32)
            upper = hi_ref[pl.ds(first_row, receivers), s : s + 1].astype(jnp.float32)
            rising = jnp.clip((axis - lower + 32.0) / 32.0, 0.0, 1.0)
            falling = jnp.clip((upper - axis) / 32.0, 0.0, 1.0)
            out_ref[s] = (rising * falling * total[:, :length]).astype(jnp.bfloat16)


def body(points_axis, shots_axis, traces, panels, aperture, window_lo, window_hi):
    count = points_axis
    rows = shots_axis // count
    i = lax.axis_index("point")
    j = lax.axis_index("shot")
    z, y = j // rows, j % rows

    def flat(i_at, z_at, y_at):
        return (z_at * rows + y_at) * count + i_at

    def send(array, where):
        pairs = [
            (flat(a, b, c), flat(*where(a, b, c)))
            for a in range(count)
            for b in range(count)
            for c in range(rows)
        ]
        return lax.ppermute(array, AXES, pairs)

    masked = traces * aperture[:, :, None].astype(traces.dtype)
    pieces = [
        send(panels, lambda a, b, c, k=k: (b, (a + k) % count, c)) for k in range(count)
    ]
    gathered = masked[None, None]
    swap = lambda a, b, c: (a, b, c ^ 1)
    gathered = jnp.concatenate([gathered, send(gathered, swap)], 1)
    far_lo, far_hi = send(window_lo, swap), send(window_hi, swap)
    bit = 1
    while bit < count:
        gathered = jnp.concatenate(
            [gathered, send(gathered, lambda a, b, c, bit=bit: (a ^ bit, b, c))], 0
        )
        bit *= 2

    order = jnp.stack([i ^ ((z - k) % count) for k in range(count)] + [y]).astype(jnp.int32)
    local_shots, local_points, length = traces.shape
    receivers = panels.shape[1]
    out = jax.ShapeDtypeStruct((local_shots, receivers, length), jnp.bfloat16)
    depth = count * local_points * LANES
    near, far = pl.pallas_call(
        functools.partial(convolve_kernel, count),
        out_shape=(out, out),
        in_specs=[pl.BlockSpec(memory_space=pltpu.SMEM)]
        + [pl.BlockSpec(memory_space=pltpu.VMEM)] * (count + 5),
        out_specs=[pl.BlockSpec(memory_space=pltpu.VMEM)] * 2,
        scratch_shapes=[
            pltpu.VMEM((length // LANES * receivers, depth), jnp.bfloat16),
            pltpu.VMEM((depth, length), jnp.bfloat16),
            pltpu.VMEM((receivers, length + WIDTH - LANES), jnp.float32),
        ],
        name="convolve",
    )(order, *pieces, gathered, window_lo, window_hi, far_lo, far_hi)
    other = send(far, swap)
    near, other = near.transpose(1, 0, 2), other.transpose(1, 0, 2)
    return jnp.where(y == 0, jnp.concatenate([near, other], 0), jnp.concatenate([other, near], 0))


def solution(mesh):
    in_specs = (
        P("shot", "point", None),
        P("point", "shot", None),
        P("shot", "point"),
        P("point", "shot"),
        P("point", "shot"),
    )
    out_specs = P("point", "shot", None)
    return jax.shard_map(
        functools.partial(body, mesh.shape["point"], mesh.shape["shot"]),
        mesh=mesh, in_specs=in_specs, out_specs=out_specs, check_vma=False,
    )
```
